32 devices in a mesh: context: 4 (over z), tensor: 2 (over core), dp: 4 (over y, x).
Axes of the slice: x: 2, y: 2, z: 4, core: 2. Of those that a mesh axis runs over, the one named last changes fastest.
Arguments:
- queries: bfloat16 [4, 3072, 2048], P('dp', 'context', 'tensor'), may hold values from -1.75 to 1.75
- keys_in: bfloat16 [4, 3072, 2048], P('dp', 'context', 'tensor'), may hold values from -1.75 to 1.75
- values: bfloat16 [4, 3072, 2048], P('dp', 'context', 'tensor'), may hold values from -48 to 48
- norm_gain: float32 [2048], P('tensor'), may hold values from 0.25 to 1.75
- segment_ids: int32 [4, 48], P('dp', 'context'), may hold values from 0 to 5, never falling along the last dimension, each value on 1 to 24 neighbouring positions
- grad_out: bfloat16 [4, 3072, 2048], P('dp', 'context', 'tensor'), may hold values from -8 to 8
Outputs:
- normed_out: bfloat16 [4, 3072, 2048], P('dp', 'context', 'tensor')
- grad_queries: bfloat16 [4, 3072, 2048], P('dp', 'context', 'tensor')
- grad_keys: bfloat16 [4, 3072, 2048], P('dp', 'context', 'tensor')
- grad_values: bfloat16 [4, 3072, 2048], P('dp', 'context', 'tensor')
- grad_gain: float32 [2048], P('tensor')
The draws below stay inside these ranges and needn't reach their ends.
Inputs may be any that keep to these rules, and one draw needn't show every extreme that they name: `segment_ids`: along each sequence the ids never fall; each id is one document.
All inputs are finite; a program needn't handle non-finite values.
Results may differ from the reference program's by a relative error of at most 0.0057.
Values sent between devices are 32-bit elements; how exact they have to be, the bound alone decides.
A program may use at most 128 MiB of HBM per device.

```python
import math
import jax
import jax.numpy as jnp
import numpy as np
from jax import lax

HEADS = 16
HD = 128
BLK = 256
SEGB = 64
WIDTH = 2048
SEQ = 3072
NBLK = 48
BATCH = 4


def draw_values(key, part):
    key_base, key_cols, key_rows = jax.random.split(key, 3)
    col_scale = jnp.exp(jax.random.uniform(key_cols, (WIDTH,), jnp.float32, math.log(0.3), math.log(3.0)))
    row_scale = jnp.exp(jax.random.uniform(key_rows, (BATCH, SEQ, 1), jnp.float32, math.log(0.4), math.log(4.0)))
    base = jnp.clip(jax.random.normal(key_base, (BATCH, SEQ, WIDTH), jnp.float32), -4.0, 4.0)
    return (base * col_scale * row_scale).astype(jnp.bfloat16)


def draw_grad_out(key, part):
    key_base = jax.random.fold_in(key, 0)
    position = (jnp.arange(SEQ, dtype=jnp.float32) + 0.5) / SEQ
    base = jnp.clip(jax.random.normal(key_base, (BATCH, SEQ, WIDTH), jnp.float32), -4.0, 4.0)
    scale = 0.5 + 1.5 * position
    result = base * scale[None, :, None]
    return result.astype(jnp.bfloat16)


def levels(stream_key, extent, cuts, least, high):
    gain = 1.0
    for dim, shards_of in cuts:
        heights = jax.random.uniform(jax.random.fold_in(jax.random.fold_in(stream_key, 6), dim), (shards_of,), jnp.float32, least / len(cuts), high / len(cuts))
        gain = gain * jnp.repeat(jnp.exp(heights), extent[dim] // shards_of).reshape((-1,) + (1,) * (len(extent) - 1 - dim))
    return gain


def split_up(amount, total, limit, lean):
    loads = [(1 << 20) // math.isqrt(rank ** lean) + 1 for rank in range(2, amount + 1)]
    spare, given = total - limit - (amount - 1), [1] * (amount - 1)
    while spare > 0:
        movable = [i for i in range(amount - 1) if given[i] < limit]
        mass, budget = sum([loads[i] for i in movable]), spare
        for i in movable:
            more = min(limit - given[i], max(1, budget * loads[i] // mass), spare)
            given[i] = given[i] + more
            spare = spare - more
    return np.array([limit] + given)


def uneven(own_key, number_of, total, bound, skew):
    if number_of == 2:
        one = jax.random.randint(own_key, (), max(1, total - bound), min(bound, total - 1) + 1)
        return jnp.stack([one, total - one])
    sizes = jnp.asarray(split_up(number_of, total, bound, skew), jnp.int32)
    pairs = (number_of - 1) // 2
    source_of, taker = sizes[1:1 + 2 * pairs:2], sizes[2:2 + 2 * pairs:2]
    slack = jnp.minimum(source_of - 1, bound - taker)
    shifted = jax.random.randint(jax.random.fold_in(own_key, 1), (pairs,), 0, 1 << 20) % (slack + 1)
    sizes = sizes.at[1:1 + 2 * pairs:2].set(source_of - shifted).at[2:2 + 2 * pairs:2].set(taker + shifted)
    return sizes[jax.random.permutation(jax.random.fold_in(own_key, 2), number_of)]


def bell_draw(key, shape, spread, reach, cuts=(), kind=jnp.bfloat16):
    factor_of = levels(key, shape, cuts, -0.22, 0.18) if cuts else 1.0
    entries = jax.random.normal(key, shape, jnp.float32) * spread * factor_of
    return jnp.minimum(jnp.maximum(entries, -reach), reach).astype(kind)


def setup_inputs(seed: int = 0) -> dict:
    splits = jax.random.split(jax.random.key(seed), 7)
    queries = bell_draw(splits[0], (BATCH, SEQ, WIDTH), 0.3, 1.75, ((0, 4), (1, 4), (2, 2)))
    keys_in = bell_draw(splits[1], (BATCH, SEQ, WIDTH), 0.3, 1.75, ((0, 4), (1, 4), (2, 2)))
    values = draw_values(jax.random.fold_in(splits[6], 71), 0)
    norm_gain = jnp.clip(1.0 + 0.15 * jax.random.normal(splits[3], (WIDTH,), jnp.float32), 0.25, 1.75)
    segment_ids = jax.vmap(lambda own: jnp.searchsorted(jnp.cumsum(uneven(own, 6, NBLK, NBLK // 2, 0)), jnp.arange(NBLK), side="right"))(jax.random.split(splits[4], BATCH)).reshape((BATCH, NBLK)).astype(jnp.int32)
    grad_out = draw_grad_out(jax.random.fold_in(splits[6], 71), 0)
    return {"queries": queries, "keys_in": keys_in, "values": values, "norm_gain": norm_gain, "segment_ids": segment_ids, "grad_out": grad_out}


def block_mask(seg_block):
    length = seg_block.shape[0]
    row_index = lax.broadcasted_iota(jnp.int32, (length, length), 0)
    col_index = lax.broadcasted_iota(jnp.int32, (length, length), 1)
    return jnp.logical_and(row_index >= col_index, seg_block[:, None] == seg_block[None, :])

def block_weights(q_block, k_block, visible):
    scores = jnp.einsum('thd,shd->hts', q_block.astype(jnp.float32), k_block.astype(jnp.float32))
    return jnp.where(visible[None], scores, 0.0).astype(jnp.bfloat16)

def forward_block(carried, block_in):
    kv_state, seg_prev = carried
    q_block, k_block, v_block, seg_block = block_in
    visible = block_mask(seg_block)
    weights = block_weights(q_block, k_block, visible)
    intra = jnp.einsum('hts,she->the', weights.astype(jnp.float32), v_block.astype(jnp.float32))
    state_bf = kv_state.astype(jnp.bfloat16)
    inter = jnp.einsum('thd,hde->the', q_block.astype(jnp.float32), state_bf.astype(jnp.float32))
    matches = (seg_block == seg_prev)[:, None, None]
    attended = intra + jnp.where(matches, inter, 0.0)
    last_seg = seg_block[-1]
    in_last = (seg_block == last_seg)[:, None, None]
    added = jnp.einsum('thd,the->hde', jnp.where(in_last, k_block.astype(jnp.float32), 0.0), v_block.astype(jnp.float32))
    new_state = jnp.where(seg_prev == last_seg, kv_state, 0.0) + added
    return ((new_state, last_seg), (attended, state_bf, seg_prev))

def backward_block(grad_state, block_in):
    q_block, k_block, v_block, seg_block, grad_block, state_bf, seg_prev = block_in
    visible = block_mask(seg_block)
    weights = block_weights(q_block, k_block, visible)
    q_f = q_block.astype(jnp.float32)
    k_f = k_block.astype(jnp.float32)
    v_f = v_block.astype(jnp.float32)
    grad_f = grad_block.astype(jnp.float32)
    grad_scores = jnp.einsum('the,she->hts', grad_f, v_f)
    grad_weights = jnp.where(visible[None], grad_scores, 0.0).astype(jnp.bfloat16).astype(jnp.float32)
    grad_bf = grad_state.astype(jnp.bfloat16).astype(jnp.float32)
    before = (seg_block == seg_prev)[:, None, None]
    after = (seg_block == seg_block[-1])[:, None, None]
    grad_q = jnp.einsum('hts,shd->thd', grad_weights, k_f) + jnp.where(before, jnp.einsum('the,hde->thd', grad_f, state_bf.astype(jnp.float32)), 0.0)
    grad_k = jnp.einsum('hts,thd->shd', grad_weights, q_f) + jnp.where(after, jnp.einsum('she,hde->shd', v_f, grad_bf), 0.0)
    grad_v = jnp.einsum('hts,the->she', weights.astype(jnp.float32), grad_f) + jnp.where(after, jnp.einsum('shd,hde->she', k_f, grad_bf), 0.0)
    added = jnp.einsum('thd,the->hde', jnp.where(before, q_f, 0.0), grad_f)
    new_grad = jnp.where(seg_prev == seg_block[-1], grad_state, 0.0) + added
    return (new_grad, (grad_q.astype(jnp.bfloat16), grad_k.astype(jnp.bfloat16), grad_v.astype(jnp.bfloat16)))

def to_blocks(array):
    return array.reshape(SEQ // BLK, BLK, HEADS, HD)

def sequence_forward(inputs):
    query_seq, key_seq, value_seq, seg_seq = inputs
    seg_blocks = seg_seq.reshape(SEQ // BLK, BLK)
    start = (jnp.zeros((HEADS, HD, HD), jnp.float32), seg_seq[0])
    final, outs_seq = lax.scan(forward_block, start, (to_blocks(query_seq), to_blocks(key_seq), to_blocks(value_seq), seg_blocks))
    attended, state_bf, seg_prev = outs_seq
    return (attended.reshape(SEQ, WIDTH), state_bf, seg_prev)

def sequence_backward(inputs):
    query_seq, key_seq, value_seq, seg_seq, grad_seq, state_bf, seg_prev = inputs
    seg_blocks = seg_seq.reshape(SEQ // BLK, BLK)
    start = jnp.zeros((HEADS, HD, HD), jnp.float32)
    final, grads = lax.scan(backward_block, start, (to_blocks(query_seq), to_blocks(key_seq), to_blocks(value_seq), seg_blocks, to_blocks(grad_seq), state_bf, seg_prev), reverse=True)
    return tuple((piece.reshape(SEQ, WIDTH) for piece in grads))

def reference(queries, keys_in, values, norm_gain, segment_ids, grad_out):
    seg_all = jnp.repeat(segment_ids, SEGB, axis=1).astype(jnp.int32)
    attended, state_bf, seg_prev = lax.map(sequence_forward, (queries, keys_in, values, seg_all))
    cotangent = grad_out.astype(jnp.float32)
    radius = jnp.sqrt(lax.optimization_barrier(jnp.mean(attended * attended, axis=2)) + 1e-06)
    normed = attended / radius[:, :, None]
    normed_out = (normed * norm_gain).astype(jnp.bfloat16)
    grad_gain = lax.optimization_barrier(jnp.sum(cotangent * normed, axis=(0, 1)))
    gained = cotangent * norm_gain
    inner = lax.optimization_barrier(jnp.sum(gained * attended, axis=2))
    grad_att = ((gained - attended * (inner / (WIDTH * radius * radius))[:, :, None]) / radius[:, :, None]).astype(jnp.bfloat16)
    grad_queries, grad_keys, grad_values = lax.map(sequence_backward, (queries, keys_in, values, seg_all, grad_att, state_bf, seg_prev))
    return (normed_out, grad_queries, grad_keys, grad_values, grad_gain)
```

```python
import functools

import jax
import jax.numpy as jnp
from jax import lax
from jax.experimental import pallas as pl
from jax.experimental.pallas import tpu as pltpu
from jax.sharding import PartitionSpec as P

HD = 128
BLK = 256
SEGB = 64
PER = BLK // SEGB
F32 = jnp.float32
BF16 = jnp.bfloat16
MESH = pl.DeviceIdType.MESH


def nn(a, b):
    return lax.dot_general(a, b, (((1,), (0,)), ((), ())), preferred_element_type=F32)


def nt(a, b):
    return lax.dot_general(a, b, (((1,), (1,)), ((), ())), preferred_element_type=F32)


def tn(a, b):
    return lax.dot_general(a, b, (((0,), (0,)), ((), ())), preferred_element_type=F32)


def flag(cond):
    return jnp.where(cond, 1.0, 0.0).astype(F32)


def spread(index, ids):
    out = jnp.full(index.shape, ids[-1], jnp.int32)
    for i in reversed(range(len(ids) - 1)):
        out = jnp.where(index < (i + 1) * SEGB, ids[i], out)
    return out


def kernel(
    nctx, ndp, heads, blocks, width,
    seg_ref, gain_ref, q_hbm, k_hbm, v_hbm, g_hbm,
    no_hbm, gq_hbm, gk_hbm, gv_hbm, gg_ref,
    qs, ks, vs, gs, no_s, gq_s, gk_s, gv_s,
    att, weights, datt, visible, mprev, mlast,
    local, state_bf, s_in, s_out, grad_local, g_in, g_out,
    sq_acc, in_acc, tile_out, tile_in, sums_out, sums_in,
    gg_part, gg_dp, gg_ctx_out, gg_ctx,
    in_sem, out_sem, fs_sem, fr_sem, bs_sem, br_sem, ts_sem, tr_sem,
    xs_sem, xr_sem, ds_sem, dr_sem, cs_sem, cr_sem,
):
    ctx = lax.axis_index("context")
    ten = lax.axis_index("tensor")
    dp = lax.axis_index("dp")
    toks = blocks * BLK
    last = nctx - 1

    def in_copy(n, src, dst, h):
        cols = pl.ds(pl.multiple_of(h * HD, HD), HD)
        return pltpu.make_async_copy(src.at[0, :, cols], dst.at[h], in_sem.at[n, h])

    def out_copy(n, src, dst, h):
        cols = pl.ds(pl.multiple_of(h * HD, HD), HD)
        return pltpu.make_async_copy(src.at[h], dst.at[0, :, cols], out_sem.at[n, h])

    ins = ((k_hbm, ks), (v_hbm, vs), (q_hbm, qs), (g_hbm, gs))
    outs = ((no_s, no_hbm), (gq_s, gq_hbm), (gk_s, gk_hbm), (gv_s, gv_hbm))

    @pl.loop(0, heads)
    def _(h):
        for n in (0, 1):
            in_copy(n, *ins[n], h).start()

    @pl.loop(0, heads)
    def _(h):
        for n in (2, 3):
            in_copy(n, *ins[n], h).start()

    barrier = pltpu.get_barrier_semaphore()
    pl.semaphore_signal(barrier, inc=1, device_id={"tensor": 1 - ten}, device_id_type=MESH)

    @pl.loop(1, ndp)
    def _(d):
        pl.semaphore_signal(
            barrier, inc=1, device_id={"dp": lax.rem(dp + d, ndp)}, device_id_type=MESH
        )

    @pl.loop(1, nctx)
    def _(d):
        pl.semaphore_signal(
            barrier, inc=1, device_id={"context": lax.rem(ctx + d, nctx)}, device_id_type=MESH
        )

    seg = [[seg_ref[0, j * PER + i] for i in range(PER)] for j in range(blocks)]
    lasts = [seg[j][-1] for j in range(blocks)]
    tile_out[...] = jnp.full((8, HD), lasts[-1], jnp.int32).astype(F32)
    rows = lax.broadcasted_iota(jnp.int32, (BLK, BLK), 0)
    cols = lax.broadcasted_iota(jnp.int32, (BLK, BLK), 1)
    rows_h = lax.broadcasted_iota(jnp.int32, (BLK, HD), 0)
    for j in range(blocks):
        same = spread(rows, seg[j]) == spread(cols, seg[j])
        visible[j] = flag(jnp.logical_and(rows >= cols, same))
        seg_h = spread(rows_h, seg[j])
        at = pl.ds(j * BLK, BLK)
        mlast[at, :] = flag(seg_h == lasts[j]).astype(BF16)
        before = seg[0][0] if j == 0 else lasts[j - 1]
        mprev[at, :] = flag(seg_h == before).astype(BF16)
    step = [flag(seg[0][0] == lasts[0])]
    for j in range(1, blocks):
        step.append(flag(lasts[j - 1] == lasts[j]))

    pl.semaphore_wait(barrier, 1 + (ndp - 1) + (nctx - 1))

    def tile_copy():
        return pltpu.make_async_remote_copy(
            tile_out, tile_in, ts_sem, tr_sem,
            device_id={"context": jnp.minimum(ctx + 1, last)}, device_id_type=MESH,
        )

    def fwd_copy(h):
        return pltpu.make_async_remote_copy(
            s_out.at[h], s_in.at[h], fs_sem.at[h], fr_sem.at[h],
            device_id={"context": jnp.minimum(ctx + 1, last)}, device_id_type=MESH,
        )

    def bwd_copy(h):
        return pltpu.make_async_remote_copy(
            g_out.at[h], g_in.at[h], bs_sem.at[h], br_sem.at[h],
            device_id={"context": jnp.maximum(ctx - 1, 0)}, device_id_type=MESH,
        )

    @pl.when(ctx < last)
    def _():
        tile_copy().start()

    @pl.when(ctx == 0)
    def _():
        s_in[...] = jnp.zeros_like(s_in)
        tile_in[...] = jnp.full((8, HD), -1.0, F32)

    @pl.when(ctx == last)
    def _():
        g_in[...] = jnp.zeros_like(g_in)

    def rows_of(j):
        return pl.ds(j * BLK, BLK)

    @pl.loop(0, heads)
    def _(h):
        for n in (0, 1):
            in_copy(n, *ins[n], h).wait()
        run = None
        for j in range(blocks):
            km = ks[h, rows_of(j), :] * mlast[rows_of(j), :]
            add = tn(km, vs[h, rows_of(j), :])
            run = add if run is None else run * step[j] + add
            local[h, j] = run

        @pl.when(jnp.logical_and(ctx == 0, ctx < last))
        def _():
            s_out[h] = local[h, blocks - 1]
            fwd_copy(h).start()

    @pl.when(ctx > 0)
    def _():
        tile_copy().wait_recv()

    match = flag(tile_in[0:1, :] == jnp.full((1, HD), seg[0][0], jnp.int32).astype(F32))
    mprev[rows_of(0), :] = (mprev[rows_of(0), :].astype(F32) * match).astype(BF16)
    reach = [match * step[0]]
    for j in range(1, blocks):
        reach.append(reach[-1] * step[j])

    sq_acc[...] = jnp.zeros_like(sq_acc)
    in_acc[...] = jnp.zeros_like(in_acc)

    @pl.loop(0, heads)
    def _(h):
        @pl.when(ctx > 0)
        def _():
            fwd_copy(h).wait_recv()

        @pl.when(jnp.logical_and(ctx > 0, ctx < last))
        def _():
            s_out[h] = local[h, blocks - 1] + s_in[h] * reach[-1]
            fwd_copy(h).start()

        for n in (2, 3):
            in_copy(n, *ins[n], h).wait()
        gain = gain_ref[pl.ds(h, 1), :]
        for j in range(blocks):
            at = rows_of(j)
            q = qs[h, at, :]
            came = s_in[h]
            state = came if j == 0 else local[h, j - 1] + came * reach[j - 1]
            state = state.astype(BF16)
            state_bf[h, j] = state
            w = (nt(q, ks[h, at, :]) * visible[j]).astype(BF16)
            weights[h, j] = w
            a = nn(w, vs[h, at, :]) + nn(q * mprev[at, :], state)
            att[h, at, :] = a
            sq_acc[at, :] += a * a
            in_acc[at, :] += a * (gs[h, at, :].astype(F32) * gain)

    groups = toks // HD
    eye = (
        lax.broadcasted_iota(jnp.int32, (HD, HD), 0) == lax.broadcasted_iota(jnp.int32, (HD, HD), 1)
    )
    for n, acc in ((0, sq_acc), (1, in_acc)):
        for i in range(groups):
            col = jnp.sum(acc[pl.ds(i * HD, HD), :], axis=1, keepdims=True)
            row = jnp.sum(
                jnp.where(eye, jnp.broadcast_to(col, (HD, HD)), 0.0), axis=0, keepdims=True
            )
            sums_out[n, pl.ds(i, 1), :] = row
    swap = pltpu.make_async_remote_copy(
        sums_out, sums_in, xs_sem, xr_sem, device_id={"tensor": 1 - ten}, device_id_type=MESH
    )
    swap.start()
    swap.wait()
    for i in range(groups):
        at = pl.ds(i * HD, HD)
        cols2 = []
        for n in (0, 1):
            row = sums_out[n, pl.ds(i, 1), :] + sums_in[n, pl.ds(i, 1), :]
            cols2.append(
                jnp.sum(
                    jnp.where(eye, jnp.broadcast_to(row, (HD, HD)), 0.0), axis=1, keepdims=True
                )
            )
        mean = cols2[0] / width + 1e-06
        radius = jnp.sqrt(mean)
        sq_acc[at, :] = jnp.broadcast_to(1.0 / radius, (HD, HD))
        in_acc[at, :] = jnp.broadcast_to(cols2[1] / (width * radius * radius), (HD, HD))

    @pl.loop(0, heads)
    def _(h):
        gain = gain_ref[pl.ds(h, 1), :]
        total = jnp.zeros((1, HD), F32)
        adds = []
        for j in range(blocks):
            at = rows_of(j)
            inv = sq_acc[at, :]
            a = att[h, at, :]
            g = gs[h, at, :].astype(F32)
            normed = a * inv
            no_s[h, at, :] = (normed * gain).astype(BF16)
            total = total + jnp.sum(g * normed, axis=0, keepdims=True)
            d = ((g * gain - a * in_acc[at, :]) * inv).astype(BF16)
            datt[h, at, :] = d
            adds.append(tn(qs[h, at, :] * mprev[at, :], d))
        gg_part[pl.ds(h, 1), :] = total
        run = None
        for j in reversed(range(blocks)):
            run = adds[j] if run is None else adds[j] + run * (match * step[0] if j == 0 else step[j])
            grad_local[h, j] = run
        out_copy(0, *outs[0], h).start()

        @pl.when(jnp.logical_and(ctx == last, ctx > 0))
        def _():
            g_out[h] = grad_local[h, 0]
            bwd_copy(h).start()

    gg_dp[dp] = gg_part[...]

    def dp_copy(to, slot):
        return pltpu.make_async_remote_copy(
            gg_part, gg_dp.at[slot], ds_sem.at[to], dr_sem.at[slot],
            device_id={"dp": to}, device_id_type=MESH,
        )

    def ctx_copy(to, slot):
        return pltpu.make_async_remote_copy(
            gg_ctx_out, gg_ctx.at[slot], cs_sem.at[to], cr_sem.at[slot],
            device_id={"context": to}, device_id_type=MESH,
        )

    @pl.loop(1, ndp)
    def _(d):
        dp_copy(lax.rem(dp + d, ndp), dp).start()

    full = [None] * (blocks + 1)
    full[blocks] = 1.0
    for j in reversed(range(blocks)):
        full[j] = full[j + 1] * (match * step[0] if j == 0 else step[j])

    @pl.loop(0, heads)
    def _(h):
        @pl.when(ctx < last)
        def _():
            bwd_copy(h).wait_recv()

        @pl.when(jnp.logical_and(ctx < last, ctx > 0))
        def _():
            g_out[h] = grad_local[h, 0] + g_in[h] * full[0]
            bwd_copy(h).start()

        came = g_in[h]
        for j in range(blocks):
            at = rows_of(j)
            grad = came if j == blocks - 1 else grad_local[h, j + 1] + came * full[j + 1]
            grad = grad.astype(BF16)
            d = datt[h, at, :]
            k = ks[h, at, :]
            v = vs[h, at, :]
            mp = mprev[at, :]
            ml = mlast[at, :]
            dw = (nt(d, v) * visible[j]).astype(BF16)
            gq = nn(dw, k) + nt(d * mp, state_bf[h, j])
            gq_s[h, at, :] = gq.astype(BF16)
            gk = tn(dw, qs[h, at, :]) + nt(v * ml, grad)
            gk_s[h, at, :] = gk.astype(BF16)
            gv = tn(weights[h, j], d) + nn(k * ml, grad)
            gv_s[h, at, :] = gv.astype(BF16)
        for n in (1, 2, 3):
            out_copy(n, *outs[n], h).start()

        @pl.when(h == heads // 2)
        def _():
            @pl.loop(1, ndp)
            def _(d):
                peer = lax.rem(dp + d, ndp)
                dp_copy(peer, peer).wait_recv()

            part = gg_dp[0]
            for i in range(1, ndp):
                part = part + gg_dp[i]
            gg_ctx_out[...] = part
            gg_ctx[ctx] = part

            @pl.loop(1, nctx)
            def _(d):
                ctx_copy(lax.rem(ctx + d, nctx), ctx).start()

    @pl.loop(1, nctx)
    def _(d):
        peer = lax.rem(ctx + d, nctx)
        ctx_copy(peer, peer).wait()

    gg_ref[...] = lax.fori_loop(
        1, nctx, lambda i, total: total + gg_ctx[i], gg_ctx[0]
    )

    @pl.loop(1, ndp)
    def _(d):
        peer = lax.rem(dp + d, ndp)
        dp_copy(peer, peer).wait_send()

    @pl.when(ctx < last)
    def _():
        tile_copy().wait_send()

        @pl.loop(0, heads)
        def _(h):
            fwd_copy(h).wait_send()

    @pl.when(ctx > 0)
    def _():
        @pl.loop(0, heads)
        def _(h):
            bwd_copy(h).wait_send()

    @pl.loop(0, heads)
    def _(h):
        for n in range(4):
            out_copy(n, *outs[n], h).wait()


def body(nctx, ndp, full_width, queries, keys_in, values, norm_gain, segment_ids, grad_out):
    toks, local_width = queries.shape[1:]
    heads = local_width // HD
    blocks = toks // BLK
    wide = jax.ShapeDtypeStruct(queries.shape, BF16)
    hbm = pl.BlockSpec(memory_space=pl.ANY)
    vmem = pl.BlockSpec(memory_space=pltpu.VMEM)
    per_head = pltpu.VMEM((heads, toks, HD), BF16)
    states = pltpu.VMEM((heads, blocks, HD, HD), F32)
    hops = pltpu.VMEM((heads, HD, HD), F32)
    rowish = pltpu.VMEM((toks, HD), F32)
    dma = pltpu.SemaphoreType.DMA
    groups = -(-(toks // HD) // 8) * 8
    sums = pltpu.VMEM((2, groups, HD), F32)
    part = pltpu.VMEM((heads, HD), F32)
    outs = pl.pallas_call(
        functools.partial(kernel, nctx, ndp, heads, blocks, full_width),
        out_shape=[wide] * 4 + [jax.ShapeDtypeStruct((heads, HD), F32)],
        in_specs=[pl.BlockSpec(memory_space=pltpu.SMEM), vmem] + [hbm] * 4,
        out_specs=[hbm] * 4 + [vmem],
        scratch_shapes=[per_head] * 8
        + [
            pltpu.VMEM((heads, toks, HD), F32),
            pltpu.VMEM((heads, blocks, BLK, BLK), BF16),
            per_head,
            pltpu.VMEM((blocks, BLK, BLK), F32),
            pltpu.VMEM((toks, HD), BF16),
            pltpu.VMEM((toks, HD), BF16),
            states,
            pltpu.VMEM((heads, blocks, HD, HD), BF16),
            hops, hops, states, hops, hops,
            rowish, rowish,
            pltpu.VMEM((8, HD), F32), pltpu.VMEM((8, HD), F32),
            sums, sums,
            part,
            pltpu.VMEM((ndp, heads, HD), F32),
            part,
            pltpu.VMEM((nctx, heads, HD), F32),
            dma((4, heads)), dma((4, heads)),
            dma((heads,)), dma((heads,)), dma((heads,)), dma((heads,)),
            dma, dma, dma, dma,
            dma((ndp,)), dma((ndp,)), dma((nctx,)), dma((nctx,)),
        ],
        compiler_params=pltpu.CompilerParams(
            collective_id=0, has_side_effects=True, vmem_limit_bytes=56 << 20
        ),
    )(segment_ids, norm_gain.reshape(heads, HD), queries, keys_in, values, grad_out)
    return (*outs[:4], outs[4].reshape(local_width))


def solution(mesh):
    wide = P("dp", "context", "tensor")
    in_specs = (wide, wide, wide, P("tensor"), P("dp", "context"), wide)
    out_specs = (wide, wide, wide, wide, P("tensor"))

    def run(queries, *rest):
        fn = functools.partial(
            body, mesh.shape["context"], mesh.shape["dp"], queries.shape[2]
        )
        return jax.shard_map(
            fn, mesh=mesh, in_specs=in_specs, out_specs=out_specs, check_vma=False
        )(queries, *rest)

    return run
```

```python
import functools

import jax
import jax.numpy as jnp
from jax import lax
from jax.experimental import pallas as pl
from jax.experimental.pallas import tpu as pltpu
from jax.sharding import PartitionSpec as P

HD = 128
BLK = 256
SEGB = 64
PER = BLK // SEGB
LAG_F = 2
LAG_B = 3
F32 = jnp.float32
BF16 = jnp.bfloat16
MESH = pl.DeviceIdType.MESH


def nn(a, b):
    return lax.dot_general(a, b, (((1,), (0,)), ((), ())), preferred_element_type=F32)


def nt(a, b):
    return lax.dot_general(a, b, (((1,), (1,)), ((), ())), preferred_element_type=F32)


def tn(a, b):
    return lax.dot_general(a, b, (((0,), (0,)), ((), ())), preferred_element_type=F32)


def flag(cond):
    return jnp.where(cond, 1.0, 0.0).astype(F32)


def spread(index, ids):
    out = jnp.full(index.shape, ids[-1], jnp.int32)
    for i in reversed(range(len(ids) - 1)):
        out = jnp.where(index < (i + 1) * SEGB, ids[i], out)
    return out


def kernel(
    nctx, ndp, heads, blocks, width,
    seg_ref, gain_ref, q_hbm, k_hbm, v_hbm, g_hbm,
    no_s, gq_s, gk_s, gv_s, gg_ref,
    qs, ks, vs, gs,
    att, gv_part, weights, visible, mprev, mlast,
    local, state_bf, s_in, s_out, grad_local, g_in, g_out,
    sq_acc, in_acc, tile_out, tile_in, sums_out, sums_in,
    gg_part, gg_dp, gg_ctx_out, gg_ctx, datt, match_ref,
    in_sem, fs_sem, fr_sem, bs_sem, br_sem, ts_sem, tr_sem,
    xs_sem, xr_sem, ds_sem, dr_sem, cs_sem, cr_sem,
):
    ctx = lax.axis_index("context")
    ten = lax.axis_index("tensor")
    dp = lax.axis_index("dp")
    toks = blocks * BLK
    last = nctx - 1

    def in_copy(n, src, dst, h):
        cols = pl.ds(pl.multiple_of(h * HD, HD), HD)
        return pltpu.make_async_copy(src.at[0, :, cols], dst.at[h], in_sem.at[n, h])

    ins = ((k_hbm, ks), (v_hbm, vs), (q_hbm, qs), (g_hbm, gs))

    @pl.loop(0, heads)
    def _(h):
        for n in (0, 1):
            in_copy(n, *ins[n], h).start()

    @pl.loop(0, heads)
    def _(h):
        for n in (2, 3):
            in_copy(n, *ins[n], h).start()

    barrier = pltpu.get_barrier_semaphore()
    pl.semaphore_signal(barrier, inc=1, device_id={"tensor": 1 - ten}, device_id_type=MESH)

    @pl.loop(1, ndp)
    def _(d):
        pl.semaphore_signal(
            barrier, inc=1, device_id={"dp": lax.rem(dp + d, ndp)}, device_id_type=MESH
        )

    @pl.loop(1, nctx)
    def _(d):
        pl.semaphore_signal(
            barrier, inc=1, device_id={"context": lax.rem(ctx + d, nctx)}, device_id_type=MESH
        )

    seg = [[seg_ref[0, j * PER + i] for i in range(PER)] for j in range(blocks)]
    lasts = [seg[j][-1] for j in range(blocks)]
    tile_out[...] = jnp.full((8, HD), lasts[-1], jnp.int32).astype(F32)
    rows = lax.broadcasted_iota(jnp.int32, (BLK, BLK), 0)
    cols = lax.broadcasted_iota(jnp.int32, (BLK, BLK), 1)
    rows_h = lax.broadcasted_iota(jnp.int32, (BLK, HD), 0)
    for j in range(blocks):
        same = spread(rows, seg[j]) == spread(cols, seg[j])
        visible[j] = flag(jnp.logical_and(rows >= cols, same))
        seg_h = spread(rows_h, seg[j])
        at = pl.ds(j * BLK, BLK)
        mlast[at, :] = flag(seg_h == lasts[j]).astype(BF16)
        before = seg[0][0] if j == 0 else lasts[j - 1]
        mprev[at, :] = flag(seg_h == before).astype(BF16)
    step = [flag(seg[0][0] == lasts[0])]
    for j in range(1, blocks):
        step.append(flag(lasts[j - 1] == lasts[j]))

    pl.semaphore_wait(barrier, 1 + (ndp - 1) + (nctx - 1))

    def tile_copy():
        return pltpu.make_async_remote_copy(
            tile_out, tile_in, ts_sem, tr_sem,
            device_id={"context": jnp.minimum(ctx + 1, last)}, device_id_type=MESH,
        )

    def fwd_copy(h):
        return pltpu.make_async_remote_copy(
            s_out.at[h], s_in.at[h], fs_sem.at[h], fr_sem.at[h],
            device_id={"context": jnp.minimum(ctx + 1, last)}, device_id_type=MESH,
        )

    def bwd_copy(h):
        return pltpu.make_async_remote_copy(
            g_out.at[h], g_in.at[h], bs_sem.at[h], br_sem.at[h],
            device_id={"context": jnp.maximum(ctx - 1, 0)}, device_id_type=MESH,
        )

    @pl.when(ctx < last)
    def _():
        tile_copy().start()

    @pl.when(ctx == 0)
    def _():
        s_in[...] = jnp.zeros_like(s_in)
        tile_in[...] = jnp.full((8, HD), -1.0, F32)

    @pl.when(ctx == last)
    def _():
        g_in[...] = jnp.zeros_like(g_in)

    def rows_of(j):
        return pl.ds(j * BLK, BLK)

    sq_acc[...] = jnp.zeros_like(sq_acc)
    in_acc[...] = jnp.zeros_like(in_acc)

    @pl.loop(0, heads + LAG_F)
    def _(i):
        @pl.when(i == LAG_F)
        def _():
            @pl.when(ctx > 0)
            def _():
                tile_copy().wait_recv()

            first = jnp.full((1, HD), seg[0][0], jnp.int32).astype(F32)
            same = flag(tile_in[0:1, :] == first)
            match_ref[...] = jnp.broadcast_to(same, (8, HD))
            at = rows_of(0)
            mprev[at, :] = (mprev[at, :].astype(F32) * same).astype(BF16)

        @pl.when(i >= LAG_F)
        def _():
            h = i - LAG_F
            match = match_ref[0:1, :]
            reach = [match * step[0]]
            for j in range(1, blocks):
                reach.append(reach[-1] * step[j])

            @pl.when(ctx > 0)
            def _():
                fwd_copy(h).wait_recv()

            @pl.when(jnp.logical_and(ctx > 0, ctx < last))
            def _():
                s_out[h] = local[h, blocks - 1] + s_in[h] * reach[-1]
                fwd_copy(h).start()

            in_copy(3, *ins[3], h).wait()
            gain = gain_ref[pl.ds(h, 1), :]
            for j in range(blocks):
                at = rows_of(j)
                came = s_in[h]
                state = came if j == 0 else local[h, j - 1] + came * reach[j - 1]
                state = state.astype(BF16)
                state_bf[h, j] = state
                a = att[h, at, :] + nn(qs[h, at, :] * mprev[at, :], state)
                att[h, at, :] = a
                sq_acc[at, :] += a * a
                in_acc[at, :] += a * (gs[h, at, :].astype(F32) * gain)

        @pl.when(i < heads)
        def _():
            h = i
            for n in (0, 1):
                in_copy(n, *ins[n], h).wait()
            run = None
            for j in range(blocks):
                km = ks[h, rows_of(j), :] * mlast[rows_of(j), :]
                add = tn(km, vs[h, rows_of(j), :])
                run = add if run is None else run * step[j] + add
                local[h, j] = run

            @pl.when(jnp.logical_and(ctx == 0, ctx < last))
            def _():
                s_out[h] = local[h, blocks - 1]
                fwd_copy(h).start()

            in_copy(2, *ins[2], h).wait()
            for j in range(blocks):
                at = rows_of(j)
                w = (nt(qs[h, at, :], ks[h, at, :]) * visible[j]).astype(BF16)
                weights[h, j] = w
                att[h, at, :] = nn(w, vs[h, at, :])

    groups = toks // HD
    eye = (
        lax.broadcasted_iota(jnp.int32, (HD, HD), 0) == lax.broadcasted_iota(jnp.int32, (HD, HD), 1)
    )
    for n, acc in ((0, sq_acc), (1, in_acc)):
        for i in range(groups):
            col = jnp.sum(acc[pl.ds(i * HD, HD), :], axis=1, keepdims=True)
            row = jnp.sum(
                jnp.where(eye, jnp.broadcast_to(col, (HD, HD)), 0.0), axis=0, keepdims=True
            )
            sums_out[n, pl.ds(i, 1), :] = row
    swap = pltpu.make_async_remote_copy(
        sums_out, sums_in, xs_sem, xr_sem, device_id={"tensor": 1 - ten}, device_id_type=MESH
    )
    swap.start()
    swap.wait()
    total_sq = sums_out[0] + sums_in[0]
    total_in = sums_out[1] + sums_in[1]
    radius = jnp.sqrt(total_sq / width + 1e-06)
    inv = 1.0 / radius
    sums_out[0] = inv
    sums_out[1] = total_in / (width * radius * radius) * inv
    for n, acc in ((0, sq_acc), (1, in_acc)):
        for i in range(groups):
            row = jnp.broadcast_to(sums_out[n, pl.ds(i, 1), :], (HD, HD))
            acc[pl.ds(i * HD, HD), :] = row.T

    def dp_copy(to, slot):
        return pltpu.make_async_remote_copy(
            gg_part, gg_dp.at[slot], ds_sem.at[to], dr_sem.at[slot],
            device_id={"dp": to}, device_id_type=MESH,
        )

    def ctx_copy(to, slot):
        return pltpu.make_async_remote_copy(
            gg_ctx_out, gg_ctx.at[slot], cs_sem.at[to], cr_sem.at[slot],
            device_id={"context": to}, device_id_type=MESH,
        )

    match = match_ref[0:1, :]
    keep = [match * step[0]] + step[1:]
    full = [None] * (blocks + 1)
    full[blocks] = 1.0
    for j in reversed(range(blocks)):
        full[j] = full[j + 1] * keep[j]

    @pl.loop(0, heads + LAG_B)
    def _(i):
        @pl.when(i == heads)
        def _():
            gg_dp[dp] = gg_part[...]

            @pl.loop(1, ndp)
            def _(d):
                dp_copy(lax.rem(dp + d, ndp), dp).start()

        @pl.when(i >= LAG_B)
        def _():
            h = i - LAG_B

            @pl.when(ctx < last)
            def _():
                bwd_copy(h).wait_recv()

            @pl.when(jnp.logical_and(ctx < last, ctx > 0))
            def _():
                g_out[h] = grad_local[h, 0] + g_in[h] * full[0]
                bwd_copy(h).start()

            came = g_in[h]
            for j in range(blocks):
                at = rows_of(j)
                grad = came if j == blocks - 1 else grad_local[h, j + 1] + came * full[j + 1]
                grad = grad.astype(BF16)
                ml = mlast[at, :]
                gk_s[h, at, :] = (att[h, at, :] + nt(vs[h, at, :] * ml, grad)).astype(BF16)
                gv_s[h, at, :] = (gv_part[h, at, :] + nn(ks[h, at, :] * ml, grad)).astype(BF16)

        @pl.when(i == heads + 1)
        def _():
            @pl.loop(1, ndp)
            def _(d):
                peer = lax.rem(dp + d, ndp)
                dp_copy(peer, peer).wait_recv()

            part = gg_dp[0]
            for n in range(1, ndp):
                part = part + gg_dp[n]
            gg_ctx_out[...] = part
            gg_ctx[ctx] = part

            @pl.loop(1, nctx)
            def _(d):
                ctx_copy(lax.rem(ctx + d, nctx), ctx).start()

        @pl.when(i < heads)
        def _():
            h = i
            gain = gain_ref[pl.ds(h, 1), :]
            total = jnp.zeros((1, HD), F32)
            adds = []
            for j in range(blocks):
                at = rows_of(j)
                inv = sq_acc[at, :]
                a = att[h, at, :]
                g = gs[h, at, :].astype(F32)
                normed = a * inv
                no_s[h, at, :] = (normed * gain).astype(BF16)
                total = total + jnp.sum(g * normed, axis=0, keepdims=True)
                d = (g * gain * inv - a * in_acc[at, :]).astype(BF16)
                datt[at, :] = d
                adds.append(tn(qs[h, at, :] * mprev[at, :], d))
            gg_part[pl.ds(h, 1), :] = total
            run = None
            for j in reversed(range(blocks)):
                run = adds[j] if run is None else adds[j] + run * keep[j]
                grad_local[h, j] = run

            @pl.when(jnp.logical_and(ctx == last, ctx > 0))
            def _():
                g_out[h] = grad_local[h, 0]
                bwd_copy(h).start()

            for j in range(blocks):
                at = rows_of(j)
                d = datt[at, :]
                dw = (nt(d, vs[h, at, :]) * visible[j]).astype(BF16)
                gq = nn(dw, ks[h, at, :]) + nt(d * mprev[at, :], state_bf[h, j])
                gq_s[h, at, :] = gq.astype(BF16)
                att[h, at, :] = tn(dw, qs[h, at, :])
                gv_part[h, at, :] = tn(weights[h, j], d)

    @pl.loop(1, nctx)
    def _(d):
        peer = lax.rem(ctx + d, nctx)
        ctx_copy(peer, peer).wait()

    gg_ref[...] = lax.fori_loop(
        1, nctx, lambda i, total: total + gg_ctx[i], gg_ctx[0]
    )

    @pl.loop(1, ndp)
    def _(d):
        peer = lax.rem(dp + d, ndp)
        dp_copy(peer, peer).wait_send()

    @pl.when(ctx < last)
    def _():
        tile_copy().wait_send()

        @pl.loop(0, heads)
        def _(h):
            fwd_copy(h).wait_send()

    @pl.when(ctx > 0)
    def _():
        @pl.loop(0, heads)
        def _(h):
            bwd_copy(h).wait_send()


def writer(heads, *refs):
    sems, gain_sem = refs[10:]
    small = pltpu.make_async_copy(refs[4], refs[9], gain_sem)
    small.start()

    def copy(n, h):
        cols = pl.ds(pl.multiple_of(h * HD, HD), HD)
        return pltpu.make_async_copy(refs[n].at[h], refs[5 + n].at[0, :, cols], sems.at[n, h])

    @pl.loop(0, heads)
    def _(h):
        for n in range(4):
            copy(n, h).start()

    @pl.loop(0, heads)
    def _(h):
        for n in range(4):
            copy(n, h).wait()

    small.wait()


def body(nctx, ndp, full_width, queries, keys_in, values, norm_gain, segment_ids, grad_out):
    toks, local_width = queries.shape[1:]
    heads = local_width // HD
    blocks = toks // BLK
    wide = jax.ShapeDtypeStruct(queries.shape, BF16)
    hbm = pl.BlockSpec(memory_space=pl.ANY)
    vmem = pl.BlockSpec(memory_space=pltpu.VMEM)
    per_head = pltpu.VMEM((heads, toks, HD), BF16)
    states = pltpu.VMEM((heads, blocks, HD, HD), F32)
    hops = pltpu.VMEM((heads, HD, HD), F32)
    rowish = pltpu.VMEM((toks, HD), F32)
    dma = pltpu.SemaphoreType.DMA
    groups = -(-(toks // HD) // 8) * 8
    sums = pltpu.VMEM((2, groups, HD), F32)
    part = pltpu.VMEM((heads, HD), F32)
    outs = pl.pallas_call(
        functools.partial(kernel, nctx, ndp, heads, blocks, full_width),
        out_shape=[pltpu.VMEM((heads, toks, HD), BF16)] * 4 + [pltpu.VMEM((heads, HD), F32)],
        in_specs=[pl.BlockSpec(memory_space=pltpu.SMEM), vmem] + [hbm] * 4,
        out_specs=[vmem] * 4 + [vmem],
        scratch_shapes=[per_head] * 4
        + [
            pltpu.VMEM((heads, toks, HD), F32),
            pltpu.VMEM((heads, toks, HD), F32),
            pltpu.VMEM((heads, blocks, BLK, BLK), BF16),
            pltpu.VMEM((blocks, BLK, BLK), F32),
            pltpu.VMEM((toks, HD), BF16),
            pltpu.VMEM((toks, HD), BF16),
            states,
            pltpu.VMEM((heads, blocks, HD, HD), BF16),
            hops, hops, states, hops, hops,
            rowish, rowish,
            pltpu.VMEM((8, HD), F32), pltpu.VMEM((8, HD), F32),
            sums, sums,
            part,
            pltpu.VMEM((ndp, heads, HD), F32),
            part,
            pltpu.VMEM((nctx, heads, HD), F32),
            pltpu.VMEM((toks, HD), BF16),
            pltpu.VMEM((8, HD), F32),
            dma((4, heads)),
            dma((heads,)), dma((heads,)), dma((heads,)), dma((heads,)),
            dma, dma, dma, dma,
            dma((ndp,)), dma((ndp,)), dma((nctx,)), dma((nctx,)),
        ],
        compiler_params=pltpu.CompilerParams(
            collective_id=0, has_side_effects=True, vmem_limit_bytes=55 << 20
        ),
    )(segment_ids, norm_gain.reshape(heads, HD), queries, keys_in, values, grad_out)
    copies = pl.pallas_call(
        functools.partial(writer, heads),
        out_shape=[wide] * 4 + [jax.ShapeDtypeStruct((heads, HD), F32)],
        in_specs=[hbm] * 5,
        out_specs=[hbm] * 5,
        scratch_shapes=[dma((4, heads)), dma],
        compiler_params=pltpu.CompilerParams(vmem_limit_bytes=1 << 20),
    )(*outs)
    return (*copies[:4], copies[4].reshape(local_width))


def solution(mesh):
    wide = P("dp", "context", "tensor")
    in_specs = (wide, wide, wide, P("tensor"), P("dp", "context"), wide)
    out_specs = (wide, wide, wide, wide, P("tensor"))

    def run(queries, *rest):
        fn = functools.partial(
            body, mesh.shape["context"], mesh.shape["dp"], queries.shape[2]
        )
        return jax.shard_map(
            fn, mesh=mesh, in_specs=in_specs, out_specs=out_specs, check_vma=False
        )(queries, *rest)

    return run
```

```python
import functools

import jax
import jax.numpy as jnp
from jax import lax
from jax.experimental import pallas as pl
from jax.experimental.pallas import tpu as pltpu
from jax.sharding import PartitionSpec as P

HD = 128
BLK = 256
SEGB = 64
PER = BLK // SEGB
F32 = jnp.float32
BF16 = jnp.bfloat16
MESH = pl.DeviceIdType.MESH


def nn(a, b):
    return lax.dot_general(a, b, (((1,), (0,)), ((), ())), preferred_element_type=F32)


def nt(a, b):
    return lax.dot_general(a, b, (((1,), (1,)), ((), ())), preferred_element_type=F32)


def tn(a, b):
    return lax.dot_general(a, b, (((0,), (0,)), ((), ())), preferred_element_type=F32)


def flag(cond):
    return jnp.where(cond, 1.0, 0.0).astype(F32)


def spread(index, ids):
    out = jnp.full(index.shape, ids[-1], jnp.int32)
    for i in reversed(range(len(ids) - 1)):
        out = jnp.where(index < (i + 1) * SEGB, ids[i], out)
    return out


def kernel(
    nctx, ndp, heads, blocks, width,
    seg_ref, gain_ref, q_hbm, k_hbm, v_hbm, g_hbm,
    no_s, gq_s, gk_s, gv_s, gg_ref,
    qs, ks, vs, gs,
    att, gv_part, weights_t, visible, visible_t, mprev, mlast,
    local, state_bf, s_in, s_out, grad_local, g_in, g_out,
    sq_acc, in_acc, tile_out, tile_in, sums_out, sums_in,
    gg_part, gg_dp, gg_ctx_out, gg_ctx, datt, match_ref,
    in_sem, fs_sem, fr_sem, bs_sem, br_sem, ts_sem, tr_sem,
    xs_sem, xr_sem, ds_sem, dr_sem, cs_sem, cr_sem,
):
    ctx = lax.axis_index("context")
    ten = lax.axis_index("tensor")
    dp = lax.axis_index("dp")
    toks = blocks * BLK
    last = nctx - 1
    lag_f = jnp.clip(3 * ctx, 2, heads)
    lag_b = jnp.clip(2 * (last - ctx), 2, heads)

    def in_copy(n, src, dst, h):
        cols = pl.ds(pl.multiple_of(h * HD, HD), HD)
        return pltpu.make_async_copy(src.at[0, :, cols], dst.at[h], in_sem.at[n, h])

    ins = ((k_hbm, ks), (v_hbm, vs), (q_hbm, qs), (g_hbm, gs))

    barrier = pltpu.get_barrier_semaphore()
    pl.semaphore_signal(barrier, inc=1, device_id={"tensor": 1 - ten}, device_id_type=MESH)

    @pl.loop(1, ndp)
    def _(d):
        pl.semaphore_signal(
            barrier, inc=1, device_id={"dp": lax.rem(dp + d, ndp)}, device_id_type=MESH
        )

    @pl.loop(1, nctx)
    def _(d):
        pl.semaphore_signal(
            barrier, inc=1, device_id={"context": lax.rem(ctx + d, nctx)}, device_id_type=MESH
        )

    @pl.loop(0, heads)
    def _(h):
        for n in (0, 1):
            in_copy(n, *ins[n], h).start()

    @pl.loop(0, heads)
    def _(h):
        for n in (2, 3):
            in_copy(n, *ins[n], h).start()

    seg = [[seg_ref[0, j * PER + i] for i in range(PER)] for j in range(blocks)]
    lasts = [seg[j][-1] for j in range(blocks)]
    tile_out[...] = jnp.full((8, HD), lasts[-1], jnp.int32).astype(F32)
    rows_h = lax.broadcasted_iota(jnp.int32, (BLK, HD), 0)
    for j in range(blocks):
        seg_h = spread(rows_h, seg[j])
        mlast[pl.ds(j * BLK, BLK), :] = flag(seg_h == lasts[j]).astype(BF16)
    step = [flag(seg[0][0] == lasts[0])]
    for j in range(1, blocks):
        step.append(flag(lasts[j - 1] == lasts[j]))

    pl.semaphore_wait(barrier, 1 + (ndp - 1) + (nctx - 1))

    def tile_copy():
        return pltpu.make_async_remote_copy(
            tile_out, tile_in, ts_sem, tr_sem,
            device_id={"context": jnp.minimum(ctx + 1, last)}, device_id_type=MESH,
        )

    def fwd_copy(h):
        return pltpu.make_async_remote_copy(
            s_out.at[h], s_in.at[h], fs_sem.at[h], fr_sem.at[h],
            device_id={"context": jnp.minimum(ctx + 1, last)}, device_id_type=MESH,
        )

    def bwd_copy(h):
        return pltpu.make_async_remote_copy(
            g_out.at[h], g_in.at[h], bs_sem.at[h], br_sem.at[h],
            device_id={"context": jnp.maximum(ctx - 1, 0)}, device_id_type=MESH,
        )

    @pl.when(ctx < last)
    def _():
        tile_copy().start()

    @pl.when(ctx == 0)
    def _():
        s_in[...] = jnp.zeros_like(s_in)
        tile_in[...] = jnp.full((8, HD), -1.0, F32)

    @pl.when(ctx == last)
    def _():
        g_in[...] = jnp.zeros_like(g_in)

    def rows_of(j):
        return pl.ds(j * BLK, BLK)

    @pl.loop(0, heads + lag_f)
    def _(i):
        @pl.when(i == lag_f)
        def _():
            @pl.when(ctx > 0)
            def _():
                tile_copy().wait_recv()

            first = jnp.full((1, HD), seg[0][0], jnp.int32).astype(F32)
            same = flag(tile_in[0:1, :] == first)
            match_ref[...] = jnp.broadcast_to(same, (8, HD))
            at = rows_of(0)
            mprev[at, :] = (mprev[at, :].astype(F32) * same).astype(BF16)

        @pl.when(i >= lag_f)
        def _():
            h = i - lag_f
            match = match_ref[0:1, :]
            reach = [match * step[0]]
            for j in range(1, blocks):
                reach.append(reach[-1] * step[j])

            @pl.when(ctx > 0)
            def _():
                fwd_copy(h).wait_recv()

            @pl.when(jnp.logical_and(ctx > 0, ctx < last))
            def _():
                s_out[h] = local[h, blocks - 1] + s_in[h] * reach[-1]
                fwd_copy(h).start()

            in_copy(3, *ins[3], h).wait()
            gain = gain_ref[pl.ds(h, 1), :]
            for j in range(blocks):
                at = rows_of(j)
                came = s_in[h]
                state = came if j == 0 else local[h, j - 1] + came * reach[j - 1]
                state = state.astype(BF16)
                state_bf[h, j] = state
                a = att[h, at, :] + nn(qs[h, at, :] * mprev[at, :], state)
                att[h, at, :] = a
                sq_acc[at, :] += a * a
                in_acc[at, :] += a * (gs[h, at, :].astype(F32) * gain)

        @pl.when(i < heads)
        def _():
            h = i
            for n in (0, 1):
                in_copy(n, *ins[n], h).wait()
            run = None
            for j in range(blocks):
                km = ks[h, rows_of(j), :] * mlast[rows_of(j), :]
                add = tn(km, vs[h, rows_of(j), :])
                run = add if run is None else run * step[j] + add
                local[h, j] = run

            @pl.when(jnp.logical_and(ctx == 0, ctx < last))
            def _():
                s_out[h] = local[h, blocks - 1]
                fwd_copy(h).start()

            @pl.when(i == 0)
            def _():
                rows = lax.broadcasted_iota(jnp.int32, (BLK, BLK), 0)
                cols = lax.broadcasted_iota(jnp.int32, (BLK, BLK), 1)
                for j in range(blocks):
                    same = spread(rows, seg[j]) == spread(cols, seg[j])
                    visible[j] = flag(jnp.logical_and(rows >= cols, same))
                    visible_t[j] = flag(jnp.logical_and(cols >= rows, same))
                    before = seg[0][0] if j == 0 else lasts[j - 1]
                    mprev[rows_of(j), :] = flag(spread(rows_h, seg[j]) == before).astype(BF16)
                sq_acc[...] = jnp.zeros_like(sq_acc)
                in_acc[...] = jnp.zeros_like(in_acc)

            in_copy(2, *ins[2], h).wait()
            for j in range(blocks):
                at = rows_of(j)
                w = (nt(qs[h, at, :], ks[h, at, :]) * visible[j]).astype(BF16)
                w_t = nt(ks[h, at, :], qs[h, at, :]) * visible_t[j]
                weights_t[h, j] = w_t.astype(BF16)
                att[h, at, :] = nn(w, vs[h, at, :])

    groups = toks // HD
    eye = (
        lax.broadcasted_iota(jnp.int32, (HD, HD), 0) == lax.broadcasted_iota(jnp.int32, (HD, HD), 1)
    )
    for n, acc in ((0, sq_acc), (1, in_acc)):
        for i in range(groups):
            col = jnp.sum(acc[pl.ds(i * HD, HD), :], axis=1, keepdims=True)
            row = jnp.sum(
                jnp.where(eye, jnp.broadcast_to(col, (HD, HD)), 0.0), axis=0, keepdims=True
            )
            sums_out[n, pl.ds(i, 1), :] = row
    swap = pltpu.make_async_remote_copy(
        sums_out, sums_in, xs_sem, xr_sem, device_id={"tensor": 1 - ten}, device_id_type=MESH
    )
    swap.start()
    swap.wait()
    total_sq = sums_out[0] + sums_in[0]
    total_in = sums_out[1] + sums_in[1]
    radius = jnp.sqrt(total_sq / width + 1e-06)
    inv = 1.0 / radius
    sums_out[0] = inv
    sums_out[1] = total_in / (width * radius * radius) * inv
    for n, acc in ((0, sq_acc), (1, in_acc)):
        for i in range(groups):
            row = jnp.broadcast_to(sums_out[n, pl.ds(i, 1), :], (HD, HD))
            acc[pl.ds(i * HD, HD), :] = row.T

    def dp_copy(to, slot):
        return pltpu.make_async_remote_copy(
            gg_part, gg_dp.at[slot], ds_sem.at[to], dr_sem.at[slot],
            device_id={"dp": to}, device_id_type=MESH,
        )

    def ctx_copy(to, slot):
        return pltpu.make_async_remote_copy(
            gg_ctx_out, gg_ctx.at[slot], cs_sem.at[to], cr_sem.at[slot],
            device_id={"context": to}, device_id_type=MESH,
        )

    match = match_ref[0:1, :]
    keep = [match * step[0]] + step[1:]
    full = [None] * (blocks + 1)
    full[blocks] = 1.0
    for j in reversed(range(blocks)):
        full[j] = full[j + 1] * keep[j]

    @pl.loop(0, heads + lag_b)
    def _(i):
        @pl.when(i == heads)
        def _():
            gg_dp[dp] = gg_part[...]

            @pl.loop(1, ndp)
            def _(d):
                dp_copy(lax.rem(dp + d, ndp), dp).start()

        @pl.when(i >= lag_b)
        def _():
            h = i - lag_b

            @pl.when(ctx < last)
            def _():
                bwd_copy(h).wait_recv()

            @pl.when(jnp.logical_and(ctx < last, ctx > 0))
            def _():
                g_out[h] = grad_local[h, 0] + g_in[h] * full[0]
                bwd_copy(h).start()

            came = g_in[h]
            for j in range(blocks):
                at = rows_of(j)
                grad = came if j == blocks - 1 else grad_local[h, j + 1] + came * full[j + 1]
                grad = grad.astype(BF16)
                ml = mlast[at, :]
                gk_s[h, at, :] = (att[h, at, :] + nt(vs[h, at, :] * ml, grad)).astype(BF16)
                gv_s[h, at, :] = (gv_part[h, at, :] + nn(ks[h, at, :] * ml, grad)).astype(BF16)

        @pl.when(i == heads + 1)
        def _():
            @pl.loop(1, ndp)
            def _(d):
                peer = lax.rem(dp + d, ndp)
                dp_copy(peer, peer).wait_recv()

            part = gg_dp[0]
            for n in range(1, ndp):
                part = part + gg_dp[n]
            gg_ctx_out[...] = part
            gg_ctx[ctx] = part

            @pl.loop(1, nctx)
            def _(d):
                ctx_copy(lax.rem(ctx + d, nctx), ctx).start()

        @pl.when(i < heads)
        def _():
            h = i
            gain = gain_ref[pl.ds(h, 1), :]
            total = jnp.zeros((1, HD), F32)
            adds = []
            for j in range(blocks):
                at = rows_of(j)
                inv = sq_acc[at, :]
                a = att[h, at, :]
                g = gs[h, at, :].astype(F32)
                normed = a * inv
                no_s[h, at, :] = (normed * gain).astype(BF16)
                total = total + jnp.sum(g * normed, axis=0, keepdims=True)
                d = (g * gain * inv - a * in_acc[at, :]).astype(BF16)
                datt[at, :] = d
                adds.append(tn(qs[h, at, :] * mprev[at, :], d))
            gg_part[pl.ds(h, 1), :] = total
            run = None
            for j in reversed(range(blocks)):
                run = adds[j] if run is None else adds[j] + run * keep[j]
                grad_local[h, j] = run

            @pl.when(jnp.logical_and(ctx == last, ctx > 0))
            def _():
                g_out[h] = grad_local[h, 0]
                bwd_copy(h).start()

            for j in range(blocks):
                at = rows_of(j)
                d = datt[at, :]
                dw = (nt(d, vs[h, at, :]) * visible[j]).astype(BF16)
                gq = nn(dw, ks[h, at, :]) + nt(d * mprev[at, :], state_bf[h, j])
                gq_s[h, at, :] = gq.astype(BF16)
                dw_t = (nt(vs[h, at, :], d) * visible_t[j]).astype(BF16)
                att[h, at, :] = nn(dw_t, qs[h, at, :])
                gv_part[h, at, :] = nn(weights_t[h, j], d)

    @pl.loop(1, nctx)
    def _(d):
        peer = lax.rem(ctx + d, nctx)
        ctx_copy(peer, peer).wait()

    gg_ref[...] = lax.fori_loop(
        1, nctx, lambda i, total: total + gg_ctx[i], gg_ctx[0]
    )

    @pl.loop(1, ndp)
    def _(d):
        peer = lax.rem(dp + d, ndp)
        dp_copy(peer, peer).wait_send()

    @pl.when(ctx < last)
    def _():
        tile_copy().wait_send()

        @pl.loop(0, heads)
        def _(h):
            fwd_copy(h).wait_send()

    @pl.when(ctx > 0)
    def _():
        @pl.loop(0, heads)
        def _(h):
            bwd_copy(h).wait_send()


def writer(heads, *refs):
    sems, gain_sem = refs[10:]
    small = pltpu.make_async_copy(refs[4], refs[9], gain_sem)
    small.start()

    def copy(n, h):
        cols = pl.ds(pl.multiple_of(h * HD, HD), HD)
        return pltpu.make_async_copy(refs[n].at[h], refs[5 + n].at[0, :, cols], sems.at[n, h])

    @pl.loop(0, heads)
    def _(h):
        for n in range(4):
            copy(n, h).start()

    @pl.loop(0, heads)
    def _(h):
        for n in range(4):
            copy(n, h).wait()

    small.wait()


def body(nctx, ndp, full_width, queries, keys_in, values, norm_gain, segment_ids, grad_out):
    toks, local_width = queries.shape[1:]
    heads = local_width // HD
    blocks = toks // BLK
    wide = jax.ShapeDtypeStruct(queries.shape, BF16)
    hbm = pl.BlockSpec(memory_space=pl.ANY)
    vmem = pl.BlockSpec(memory_space=pltpu.VMEM)
    per_head = pltpu.VMEM((heads, toks, HD), BF16)
    states = pltpu.VMEM((heads, blocks, HD, HD), F32)
    hops = pltpu.VMEM((heads, HD, HD), F32)
    rowish = pltpu.VMEM((toks, HD), F32)
    dma = pltpu.SemaphoreType.DMA
    groups = -(-(toks // HD) // 8) * 8
    sums = pltpu.VMEM((2, groups, HD), F32)
    part = pltpu.VMEM((heads, HD), F32)
    outs = pl.pallas_call(
        functools.partial(kernel, nctx, ndp, heads, blocks, full_width),
        out_shape=[pltpu.VMEM((heads, toks, HD), BF16)] * 4 + [pltpu.VMEM((heads, HD), F32)],
        in_specs=[pl.BlockSpec(memory_space=pltpu.SMEM), vmem] + [hbm] * 4,
        out_specs=[vmem] * 4 + [vmem],
        scratch_shapes=[per_head] * 4
        + [
            pltpu.VMEM((heads, toks, HD), F32),
            pltpu.VMEM((heads, toks, HD), F32),
            pltpu.VMEM((heads, blocks, BLK, BLK), BF16),
            pltpu.VMEM((blocks, BLK, BLK), F32),
            pltpu.VMEM((blocks, BLK, BLK), F32),
            pltpu.VMEM((toks, HD), BF16),
            pltpu.VMEM((toks, HD), BF16),
            states,
            pltpu.VMEM((heads, blocks, HD, HD), BF16),
            hops, hops, states, hops, hops,
            rowish, rowish,
            pltpu.VMEM((8, HD), F32), pltpu.VMEM((8, HD), F32),
            sums, sums,
            part,
            pltpu.VMEM((ndp, heads, HD), F32),
            part,
            pltpu.VMEM((nctx, heads, HD), F32),
            pltpu.VMEM((toks, HD), BF16),
            pltpu.VMEM((8, HD), F32),
            dma((4, heads)),
            dma((heads,)), dma((heads,)), dma((heads,)), dma((heads,)),
            dma, dma, dma, dma,
            dma((ndp,)), dma((ndp,)), dma((nctx,)), dma((nctx,)),
        ],
        compiler_params=pltpu.CompilerParams(
            collective_id=0, has_side_effects=True, vmem_limit_bytes=55 << 20
        ),
    )(segment_ids, norm_gain.reshape(heads, HD), queries, keys_in, values, grad_out)
    copies = pl.pallas_call(
        functools.partial(writer, heads),
        out_shape=[wide] * 4 + [jax.ShapeDtypeStruct((heads, HD), F32)],
        in_specs=[hbm] * 5,
        out_specs=[hbm] * 5,
        scratch_shapes=[dma((4, heads)), dma],
        compiler_params=pltpu.CompilerParams(vmem_limit_bytes=1 << 20),
    )(*outs)
    return (*copies[:4], copies[4].reshape(local_width))


def solution(mesh):
    wide = P("dp", "context", "tensor")
    in_specs = (wide, wide, wide, P("tensor"), P("dp", "context"), wide)
    out_specs = (wide, wide, wide, wide, P("tensor"))

    def run(queries, *rest):
        fn = functools.partial(
            body, mesh.shape["context"], mesh.shape["dp"], queries.shape[2]
        )
        return jax.shard_map(
            fn, mesh=mesh, in_specs=in_specs, out_specs=out_specs, check_vma=False
        )(queries, *rest)

    return run
```
